32 devices in a mesh: groups: 2 (over x), seq: 16 (over z, y, core).
Axes of the slice: x: 2, y: 2, z: 4, core: 2. Of those that a mesh axis runs over, the one named last changes fastest.
Arguments:
- hidden: bfloat16 [8192, 2048], P(('groups', 'seq')), parts along dimension 0, may hold values from -6 to 6
- conv_weight: float32 [3, 2048], replicated, may hold values from -1.8 to 1.8
- feat_query_w: bfloat16 [2048, 256], replicated, may hold values from -0.125 to 0.125
- feat_key_w: bfloat16 [2048, 256], replicated, may hold values from -0.125 to 0.125
- win_query: bfloat16 [8192, 2048], P(('groups', 'seq')), parts along dimension 0, may hold values from -48 to 48
- win_key: bfloat16 [8192, 2048], P(('groups', 'seq')), parts along dimension 0, may hold values from -48 to 48
Outputs:
- mixed: bfloat16 [8192, 2048], P(('groups', 'seq')), parts along dimension 0
The draws below stay inside these ranges and needn't reach their ends.
There are 2 independent parts, one for each index of `groups`. The reference program is written for one: setup_inputs(seed, part) draws one part's arguments, and reference() takes and returns one part's arrays. A program takes and returns all parts, laid end to end along the dimension named above; an argument that names none is the same for every part. Nothing has to cross between parts.
All inputs are finite; a program needn't handle non-finite values.
Results may differ from the reference program's by a relative error of at most 0.008.
Values may be sent and summed in bfloat16 or wider, within the bound.
A program may use at most 192 MiB of HBM per device.

```python
import jax
import jax.numpy as jnp
from jax import lax

D = 2048
HEADS = 16
HEAD = 128
FEATURE_DIM = 16
WINDOW = 64
TOK_DEV = 256
SEQ_LEN = 4096
PHI = 273
N_SEQ = 16


def window_pair(key):
    first, second = jax.random.split(jax.random.fold_in(key, 7), 2)
    keys = jax.random.normal(first, (SEQ_LEN, D), jnp.float32)
    queries = jax.random.normal(second, (SEQ_LEN, D), jnp.float32)
    keys = jnp.clip(keys, -48.0, 48.0)
    queries = jnp.clip(queries, -48.0, 48.0)
    return (queries, keys)


def draw_win_query(key, part):
    return window_pair(key)[0].astype(jnp.bfloat16)


def draw_win_key(key, part):
    return window_pair(key)[1].astype(jnp.bfloat16)


def level_of(rng, extent, cuts, least, high):
    loudness = 1.0
    for axis_at, blocks in cuts:
        heights = jax.random.uniform(jax.random.fold_in(jax.random.fold_in(rng, 6), axis_at), (blocks,), jnp.float32, least / len(cuts), high / len(cuts))
        loudness = loudness * jnp.repeat(jnp.exp(heights), extent[axis_at] // blocks).reshape((-1,) + (1,) * (len(extent) - 1 - axis_at))
    return loudness


def scatter_about(stream_key, extent, spread, bound, shards=(), kind=jnp.bfloat16):
    values = jax.random.normal(stream_key, extent, jnp.float32) * spread
    if len(shards) > 0:
        values = level_of(stream_key, extent, shards, -0.22, 0.18) * values
    return jnp.clip(values, min=-bound, max=bound).astype(kind)


def setup_inputs(seed: int = 0, part: int = 0) -> dict:
    key_list = jax.random.split(jax.random.key(seed), 7)
    own_keys = jax.random.split(jax.random.fold_in(key_list[6], part), 7)
    return {
        "hidden": scatter_about(own_keys[0], (SEQ_LEN, D), 1.0, 6.0, ((0, 16),)),
        "conv_weight": scatter_about(key_list[1], (3, D), 0.6, 1.8, (), jnp.float32),
        "feat_query_w": scatter_about(key_list[2], (D, HEADS * FEATURE_DIM), D ** -0.5, 0.125),
        "feat_key_w": scatter_about(key_list[3], (D, HEADS * FEATURE_DIM), D ** -0.5, 0.125),
        "win_query": draw_win_query(jax.random.fold_in(jax.random.fold_in(key_list[6], part), 71), part),
        "win_key": draw_win_key(jax.random.fold_in(jax.random.fold_in(key_list[6], part), 71), part),
    }


def conv_rows(extended, conv_weight):
    wide = extended.astype(jnp.float32)
    total = conv_weight[0] * wide[:-2] + conv_weight[1] * wide[1:-1] + conv_weight[2] * wide[2:]
    return total.astype(jnp.bfloat16)


def taylor(features, heads):
    count = features.shape[0]
    wide = features.astype(jnp.float32).reshape(count, heads, -1)
    width = wide.shape[-1]
    first = wide * (width ** -0.25)
    second = jnp.repeat(wide, width, axis=-1) * jnp.tile(wide, (1, 1, width)) * ((width ** -0.5) / (2.0 ** 0.5))
    ones = jnp.ones((count, heads, 1), jnp.float32)
    return jnp.concatenate([ones, first, second], axis=-1).astype(jnp.bfloat16)


def mix_block(conv_blk, fq_blk, fk_blk, query, keys_ext, vals_ext, state, norm, start, heads):
    count, width = conv_blk.shape
    head = width // heads
    margin = keys_ext.shape[0] - count
    qh = query.astype(jnp.float32).reshape(count, heads, head)
    kh = keys_ext.astype(jnp.float32).reshape(count + margin, heads, head)
    vh = vals_ext.astype(jnp.float32).reshape(count + margin, heads, head)
    scores = jnp.einsum('qhd,khd->hqk', qh, kh) * (head ** -0.5)
    rows = jnp.arange(count, dtype=jnp.int32)[:, None]
    cols = jnp.arange(count + margin, dtype=jnp.int32)[None, :]
    allowed = (cols > rows) & (cols <= rows + margin) & (cols - margin + start >= 0)
    scores = jnp.where(allowed[None], scores, -jnp.inf)
    top = jnp.max(scores, axis=-1, keepdims=True)
    weights = jnp.exp(scores - top)
    probs = (weights / jnp.sum(weights, axis=-1, keepdims=True)).astype(jnp.bfloat16)
    y_win = jnp.einsum('hqk,khd->qhd', probs.astype(jnp.float32), vh)
    feature_map = fq_blk.shape[1] // heads
    feature_query_head = fq_blk.astype(jnp.float32).reshape(count, heads, feature_map)
    feature_key_head = fk_blk.astype(jnp.float32).reshape(count, heads, feature_map)
    inner_product = jnp.einsum('egz,tgz->get', feature_query_head, feature_key_head) * (feature_map ** -0.5)
    taylor_w = 1.0 + inner_product + 0.5 * inner_product * inner_product
    causal = jnp.arange(count, dtype=jnp.int32)[None, :] <= jnp.arange(count, dtype=jnp.int32)[:, None]
    taylor_w = jnp.where(causal[None], taylor_w, 0.0)
    den_in = jnp.sum(taylor_w, axis=-1)
    local_values = conv_blk.astype(jnp.float32).reshape(count, heads, head)
    num_in = jnp.einsum('hqk,khd->qhd', taylor_w.astype(jnp.bfloat16).astype(jnp.float32), local_values)
    phq = taylor(fq_blk, heads).astype(jnp.float32)
    num_out = jnp.einsum('qhf,hfd->qhd', phq, state, precision=lax.Precision.HIGHEST)
    den_out = jnp.einsum('qhf,hf->qh', phq, norm, precision=lax.Precision.HIGHEST)
    y_lin = (num_in + num_out) / (den_in.T + den_out)[..., None]
    return (y_win + y_lin).reshape(count, width).astype(jnp.bfloat16)


def block_state(conv_blk, fk_blk, heads):
    count, width = conv_blk.shape
    expanded_keys = taylor(fk_blk, heads).astype(jnp.float32)
    local_values = conv_blk.astype(jnp.float32).reshape(count, heads, width // heads)
    return jnp.einsum('jeq,jei->eqi', expanded_keys, local_values), jnp.sum(expanded_keys, axis=0)


def reference(hidden, conv_weight, feat_query_w, feat_key_w, win_query, win_key):
    width = hidden.shape[1]
    zeros_two = jnp.zeros((2, width), jnp.bfloat16)
    conv = conv_rows(jnp.concatenate([zeros_two, hidden], axis=0), conv_weight)
    fq = jnp.dot(conv, feat_query_w, preferred_element_type=jnp.float32).astype(jnp.bfloat16)
    fk = jnp.dot(conv, feat_key_w, preferred_element_type=jnp.float32).astype(jnp.bfloat16)
    pad = jnp.zeros((WINDOW, width), jnp.bfloat16)
    keys_pad = jnp.concatenate([pad, win_key], axis=0)
    vals_pad = jnp.concatenate([pad, conv], axis=0)
    init = (jnp.zeros((HEADS, PHI, HEAD), jnp.float32), jnp.zeros((HEADS, PHI), jnp.float32))

    def step(carry, block):
        state, norm = carry
        start = (block * TOK_DEV).astype(jnp.int32)
        conv_blk = lax.dynamic_slice_in_dim(conv, start, TOK_DEV, 0)
        fq_blk = lax.dynamic_slice_in_dim(fq, start, TOK_DEV, 0)
        fk_blk = lax.dynamic_slice_in_dim(fk, start, TOK_DEV, 0)
        query = lax.dynamic_slice_in_dim(win_query, start, TOK_DEV, 0)
        keys_ext = lax.dynamic_slice_in_dim(keys_pad, start, TOK_DEV + WINDOW, 0)
        vals_ext = lax.dynamic_slice_in_dim(vals_pad, start, TOK_DEV + WINDOW, 0)
        out = mix_block(conv_blk, fq_blk, fk_blk, query, keys_ext, vals_ext, state, norm, start, HEADS)
        key_value_state, ksum = block_state(conv_blk, fk_blk, HEADS)
        return (state + key_value_state, norm + ksum), out

    carry, outs = lax.scan(step, init, jnp.arange(N_SEQ, dtype=jnp.int32))
    return outs.reshape(SEQ_LEN, width)
```

```python
import functools

import jax
import jax.numpy as jnp
import numpy as np
from jax import lax
from jax.experimental import pallas as pl
from jax.experimental.pallas import tpu as pltpu
from jax.sharding import PartitionSpec as P

HEADS = 16
FEAT = 16
WINDOW = 64
TEAM = 4
ROWS = 160
QUADS = 136
C2 = (FEAT**-0.5) / 2.0**0.5
BF = jnp.bfloat16
F32 = jnp.float32


def tables(block):
    pairs = [(i, j) for i in range(FEAT) for j in range(i, FEAT)]
    left_k = np.zeros((2 * ROWS, 2 * FEAT), np.float32)
    reps = block // FEAT
    sel_q = np.zeros((FEAT, 512), np.float32)
    rows_q = np.zeros((8, 256), np.float32)
    for f, (i, j) in enumerate(pairs):
        left_k[f, i] = 1.0
        left_k[ROWS + f, j] = 1.0
        sel_q[i, f] = 1.0
        sel_q[j, 256 + f] = 1.0
        rows_q[2, f] = np.float32(C2) * (1.0 if i == j else 2.0)
    for i in range(FEAT):
        f = QUADS + i
        left_k[f, i] = 1.0
        left_k[ROWS + f, FEAT] = 0.5
        sel_q[i, f] = 1.0
        rows_q[1, f] = 0.5
        rows_q[2, f] = 1.0
    f = QUADS + FEAT
    left_k[f, FEAT] = 1.0
    left_k[ROWS + f, FEAT] = 1.0
    rows_q[0, f] = 1.0
    rows_q[1, f] = 1.0
    rows_q[2, f] = 1.0
    return jnp.asarray(left_k, BF), jnp.asarray(np.tile(sel_q, (reps, 1)), BF), jnp.asarray(rows_q, F32)


def nt(a, b):
    return lax.dot_general(a, b, (((1,), (1,)), ((), ())), preferred_element_type=F32)


def nn(a, b):
    return jnp.dot(a, b, preferred_element_type=F32)


def kernel(
    n, hid, cw, wq, wk, qry, key, selk, selq, rowq, out,
    hprev, kprev, vprev, cv, fqs, fkt, st, rbuf, total, cin, cout, obuf, sbuf,
    ywin, num, den, wbias, cmask,
    hs_send, hs_recv, a_send, a_recv, c_send, c_recv, b_send, b_recv,
):
    count, width = hid.shape
    head = width // HEADS
    per = HEADS // TEAM
    me = lax.axis_index("seq")
    team = me // TEAM
    pos = lax.rem(me, TEAM)
    teams = n // TEAM
    has_prev, has_next = me > 0, me < n - 1
    has_up, has_down = team > 0, team < teams - 1
    base_dev = team * TEAM

    def peer(d):
        return base_dev + lax.rem(pos + d, TEAM)

    barrier = pltpu.get_barrier_semaphore()

    def hello(dev):
        pl.semaphore_signal(barrier, inc=1, device_id={"seq": dev}, device_id_type=pl.DeviceIdType.MESH)

    for d in range(1, TEAM):
        hello(peer(d))
    pl.when(has_prev)(lambda: hello(me - 1))
    pl.when(has_next)(lambda: hello(me + 1))
    pl.when(has_up)(lambda: hello(me - TEAM))
    pl.when(has_down)(lambda: hello(me + TEAM))
    greeted = TEAM - 1
    for there in (has_prev, has_next, has_up, has_down):
        greeted = greeted + there.astype(jnp.int32)
    pl.semaphore_wait(barrier, greeted)

    def remote(src, dst, send, recv, dev):
        return pltpu.make_async_remote_copy(
            src_ref=src, dst_ref=dst, send_sem=send, recv_sem=recv,
            device_id={"seq": dev}, device_id_type=pl.DeviceIdType.MESH,
        )

    tail_copy = remote(hid.at[pl.ds(count - 16, 16)], hprev, hs_send.at[0], hs_recv.at[0], me + 1)
    key_copy = remote(key.at[pl.ds(count - WINDOW, WINDOW)], kprev, hs_send.at[1], hs_recv.at[1], me + 1)
    val_copy = remote(cv.at[pl.ds(count - WINDOW, WINDOW)], vprev, hs_send.at[2], hs_recv.at[2], me + 1)

    @pl.when(has_next)
    def _():
        tail_copy.start()
        key_copy.start()

    @pl.when(jnp.logical_not(has_prev))
    def _():
        hprev[...] = jnp.zeros_like(hprev)
        kprev[...] = jnp.zeros_like(kprev)
        vprev[...] = jnp.zeros_like(vprev)

    r = lax.broadcasted_iota(jnp.int32, (count, head), 0)
    j = lax.broadcasted_iota(jnp.int32, (count, head), 1)
    rr = lax.rem(r, WINDOW)
    first = jnp.where(has_prev, 0, WINDOW)
    ok = (j > rr) & (j <= rr + WINDOW) & ((j >= first) | (r >= WINDOW))
    wbias[...] = jnp.where(ok, 0.0, -1e30)
    r = lax.broadcasted_iota(jnp.int32, (count, count), 0)
    j = lax.broadcasted_iota(jnp.int32, (count, count), 1)
    cmask[...] = jnp.where(j <= r, 1.0, 0.0)

    pl.when(has_prev)(lambda: tail_copy.wait_recv())

    row = lax.broadcasted_iota(jnp.int32, (count, head), 0)

    def conv_step(b, c):
        cols = pl.ds(pl.multiple_of(b * head, head), head)
        h = hid[:, cols].astype(F32)
        hp = hprev[:, cols].astype(F32)
        w = cw[:, cols]
        h1 = jnp.where(row == 0, hp[15:16], pltpu.roll(h, 1, 0))
        h2 = jnp.where(row == 0, hp[14:15], jnp.where(row == 1, hp[15:16], pltpu.roll(h, 2, 0)))
        cv[:, cols] = (w[0:1] * h2 + w[1:2] * h1 + w[2:3] * h).astype(BF)
        return c

    lax.fori_loop(0, HEADS, conv_step, 0)
    pl.when(has_next)(lambda: val_copy.start())

    fk = nn(cv[...], wk[...]).astype(BF).astype(F32)
    fkt[...] = fk.T.astype(BF)

    trow = lax.broadcasted_iota(jnp.int32, (16, count), 0)
    pick_a = jnp.where(trow == 9, 1.0, 0.0).astype(BF)
    pick_b = jnp.where(trow == 10, 1.0, 0.0).astype(BF)
    ones_k = jnp.ones((FEAT, count), BF)
    zeros_k = jnp.zeros((256 - ROWS, count), BF)

    def state_step(h, c):
        x = jnp.concatenate([fkt[pl.ds(pl.multiple_of(h * FEAT, FEAT), FEAT), :], ones_k], axis=0)
        ab = nn(selk[...], x)
        p = ab[:ROWS] * ab[ROWS:]
        p = jnp.concatenate([p[:QUADS] * C2, p[QUADS:]], axis=0).astype(BF)
        v = cv[:, pl.ds(pl.multiple_of(h * head, head), head)]
        s = nn(p, v)
        tail = s[144:] + nt(pick_a, p[:128]) + nt(pick_b, jnp.concatenate([p[128:], zeros_k], axis=0))
        st[h] = jnp.concatenate([s[:144], tail], axis=0).astype(BF)
        return c

    a_copies = []
    for d in range(1, TEAM):
        p_d = lax.rem(pos + d, TEAM)
        lax.fori_loop(0, per, lambda k, c, p_d=p_d: state_step(p_d * per + k, c), 0)
        copy = remote(st.at[pl.ds(p_d * per, per)], rbuf.at[pos], a_send.at[d], a_recv.at[d], peer(d))
        copy.start()
        a_copies.append(copy)
    lax.fori_loop(0, per, lambda k, c: state_step(pos * per + k, c), 0)

    fq = nn(cv[...], wq[...]).astype(BF)
    for b in range(2):
        fqs[b] = fq[:, b * 128 : (b + 1) * 128]

    ones_v = jnp.ones((count, head), BF)
    lane = lax.broadcasted_iota(jnp.int32, (8, 128), 1)

    def masked_query(h):
        mask = jnp.where(lane // FEAT == lax.rem(h, 8), 1.0, 0.0)[0:1].astype(BF)
        return fqs[h // 8] * mask

    def local_step(h, c):
        cols = pl.ds(pl.multiple_of(h * head, head), head)
        q = qry[:, cols]
        k = jnp.concatenate([kprev[:, cols], key[:, cols]], axis=0)
        v = cv[:, cols]
        ve = jnp.concatenate([vprev[:, cols], v], axis=0)
        s = jnp.concatenate(
            [nt(q[i : i + WINDOW], k[i : i + 2 * WINDOW]) for i in range(0, count, WINDOW)], axis=0
        )
        s = s * head**-0.5 + wbias[...]
        w = jnp.exp(s - jnp.max(s, axis=-1, keepdims=True)).astype(BF)
        va = jnp.concatenate([ve, jnp.ones_like(ve)], axis=1)
        y = jnp.concatenate(
            [nn(w[i : i + WINDOW], va[i : i + 2 * WINDOW]) for i in range(0, count, WINDOW)], axis=0
        )
        ywin[:, cols] = y[:, :head] / y[:, head:]
        fqm = masked_query(h)
        x = nn(fqm, fkt[pl.ds(pl.multiple_of((h // 8) * 128, 128), 128), :]) * FEAT**-0.5
        a = ((1.0 + x + 0.5 * x * x) * cmask[...]).astype(BF)
        na = nn(a, jnp.concatenate([v, ones_v], axis=1))
        num[:, cols] = na[:, :head]
        den[:, cols] = na[:, head:]
        return c

    def collect():
        rbuf[pos] = st[pl.ds(pos * per, per)]
        for copy in a_copies:
            copy.wait_recv()
        total[...] = (
            rbuf[0].astype(F32) + rbuf[1].astype(F32) + rbuf[2].astype(F32) + rbuf[3].astype(F32)
        )

    chain = remote(cout, cin, c_send, c_recv, me + TEAM)
    b_copies = [
        remote(obuf.at[d], sbuf.at[pos], b_send.at[d], b_recv.at[d], peer(d)) for d in range(1, TEAM)
    ]

    def pass_on():
        pl.when(has_up)(lambda: chain.wait_recv())

        @pl.when(jnp.logical_not(has_up))
        def _():
            cin[...] = jnp.zeros_like(cin)

        @pl.when(has_down)
        def _():
            cout[...] = (cin[...].astype(F32) + total[...]).astype(BF)
            chain.start()

        base = cin[...].astype(F32)
        for d in range(TEAM):
            target = lax.rem(pos + d, TEAM)
            acc = base
            for i in range(TEAM - 1):
                acc = acc + rbuf[i].astype(F32) * jnp.where(i < target, 1.0, 0.0)
            if d == 0:
                sbuf[pos] = acc.astype(BF)
            else:
                obuf[d] = acc.astype(BF)
                b_copies[d - 1].start()

    pl.when(has_prev)(lambda: key_copy.wait_recv())
    pl.when(has_prev)(lambda: val_copy.wait_recv())
    lax.fori_loop(0, 4, local_step, 0)
    collect()
    turn = jnp.minimum(4 + 4 * team, HEADS - 1)

    def local_and_pass(h, c):
        pl.when(h == turn)(pass_on)
        return local_step(h, c)

    lax.fori_loop(4, HEADS, local_and_pass, 0)
    for copy in b_copies:
        copy.wait_recv()

    spare = jnp.zeros((256 - ROWS, head), BF)

    def final_step(h, c):
        cols = pl.ds(pl.multiple_of(h * head, head), head)
        lr = nn(masked_query(h), selq[...])
        ph = (((lr[:, :256] + rowq[0:1]) * (lr[:, 256:] + rowq[1:2])) * rowq[2:3]).astype(BF)
        s = sbuf[h // per, lax.rem(h, per)]
        t = s[144:].astype(F32)
        nrow = jnp.concatenate(
            [jnp.broadcast_to(t[9:10], (head, head)), jnp.broadcast_to(t[10:11], (head, head))], axis=1
        ).astype(BF)
        no = nn(ph, jnp.concatenate([s, spare], axis=0))
        do = nt(ph, nrow)
        y = ywin[:, cols] + (num[:, cols] + no) / (den[:, cols] + do)
        out[:, cols] = y.astype(BF)
        return c

    lax.fori_loop(0, HEADS, final_step, 0)

    @pl.when(has_next)
    def _():
        tail_copy.wait_send()
        key_copy.wait_send()
        val_copy.wait_send()

    for copy in a_copies + b_copies:
        copy.wait_send()
    pl.when(has_down)(lambda: chain.wait_send())


def local(n, hidden, conv_weight, feat_query_w, feat_key_w, win_query, win_key):
    count, width = hidden.shape
    head = width // HEADS
    per = HEADS // TEAM
    selk, selq, rowq = tables(128)
    quarter = (per, ROWS, head)
    dma = pltpu.SemaphoreType.DMA
    return pl.pallas_call(
        functools.partial(kernel, n),
        out_shape=jax.ShapeDtypeStruct((count, width), BF),
        in_specs=[pl.BlockSpec(memory_space=pltpu.VMEM)] * 9,
        out_specs=pl.BlockSpec(memory_space=pltpu.VMEM),
        scratch_shapes=[
            pltpu.VMEM((16, width), BF),
            pltpu.VMEM((WINDOW, width), BF),
            pltpu.VMEM((WINDOW, width), BF),
            pltpu.VMEM((count, width), BF),
            pltpu.VMEM((2, count, 128), BF),
            pltpu.VMEM((256, count), BF),
            pltpu.VMEM((HEADS, ROWS, head), BF),
            pltpu.VMEM((TEAM,) + quarter, BF),
            pltpu.VMEM(quarter, F32),
            pltpu.VMEM(quarter, BF),
            pltpu.VMEM(quarter, BF),
            pltpu.VMEM((TEAM,) + quarter, BF),
            pltpu.VMEM((TEAM,) + quarter, BF),
            pltpu.VMEM((count, width), F32),
            pltpu.VMEM((count, width), F32),
            pltpu.VMEM((count, width), F32),
            pltpu.VMEM((count, head), F32),
            pltpu.VMEM((count, count), F32),
            dma((3,)), dma((3,)), dma((TEAM,)), dma((TEAM,)), dma, dma, dma((TEAM,)), dma((TEAM,)),
        ],
        compiler_params=pltpu.CompilerParams(
            collective_id=0, has_side_effects=True, vmem_limit_bytes=48 * 1024 * 1024
        ),
    )(hidden, conv_weight, feat_query_w, feat_key_w, win_query, win_key, selk, selq, rowq)


def solution(mesh):
    placed = (P(("groups", "seq"), None), P(), P(), P(), P(("groups", "seq"), None), P(("groups", "seq"), None))
    return jax.shard_map(
        functools.partial(local, mesh.shape["seq"]),
        mesh=mesh, in_specs=placed, out_specs=P(("groups", "seq"), None), check_vma=False,
    )
```

```python
import functools

import jax
import jax.numpy as jnp
import numpy as np
from jax import lax
from jax.experimental import pallas as pl
from jax.experimental.pallas import tpu as pltpu
from jax.sharding import PartitionSpec as P

HEADS = 16
FEAT = 16
WINDOW = 64
TEAM = 4
ROWS = 160
QUADS = 136
CHUNKS = 2
TURN0 = 1
TURNC = 1
TURNT = 2
C2 = (FEAT**-0.5) / 2.0**0.5
BF = jnp.bfloat16
F32 = jnp.float32


def tables(block):
    pairs = [(i, j) for i in range(FEAT) for j in range(i, FEAT)]
    left_k = np.zeros((2 * ROWS, 2 * FEAT), np.float32)
    reps = block // FEAT
    sel_q = np.zeros((FEAT, 512), np.float32)
    rows_q = np.zeros((8, 256), np.float32)
    for f, (i, j) in enumerate(pairs):
        left_k[f, i] = 1.0
        left_k[ROWS + f, j] = 1.0
        sel_q[i, f] = 1.0
        sel_q[j, 256 + f] = 1.0
        rows_q[2, f] = np.float32(C2) * (1.0 if i == j else 2.0)
    for i in range(FEAT):
        f = QUADS + i
        left_k[f, i] = 1.0
        left_k[ROWS + f, FEAT] = 0.5
        sel_q[i, f] = 1.0
        rows_q[1, f] = 0.5
        rows_q[2, f] = 1.0
    f = QUADS + FEAT
    left_k[f, FEAT] = 1.0
    left_k[ROWS + f, FEAT] = 1.0
    rows_q[0, f] = 1.0
    rows_q[1, f] = 1.0
    rows_q[2, f] = 1.0
    return jnp.asarray(left_k, BF), jnp.asarray(np.tile(sel_q, (reps, 1)), BF), jnp.asarray(rows_q, F32)


def nt(a, b):
    return lax.dot_general(a, b, (((1,), (1,)), ((), ())), preferred_element_type=F32)


def nn(a, b):
    return jnp.dot(a, b, preferred_element_type=F32)


def kernel(
    n, hid_h, cw_h, wq_h, wk_h, qry_h, key_h, selk_h, selq_h, rowq_h, out,
    hid, cw, wq, wk, qry, key, selk, selq, rowq,
    hprev, kprev, vprev, cv, fqs, fkt, st, rbuf, cin, cout, obuf, sbuf,
    ywin, num, den, wbias, cmask,
    loads, hs_send, hs_recv, a_send, a_recv, c_send, c_recv, b_send, b_recv,
):
    count, width = hid.shape
    head = width // HEADS
    per = HEADS // TEAM
    me = lax.axis_index("seq")
    team = me // TEAM
    pos = lax.rem(me, TEAM)
    teams = n // TEAM
    has_prev, has_next = me > 0, me < n - 1
    has_up, has_down = team > 0, team < teams - 1
    base_dev = team * TEAM

    def peer(d):
        return base_dev + lax.rem(pos + d, TEAM)

    pairs = (
        (hid_h, hid), (cw_h, cw), (wk_h, wk), (selk_h, selk), (wq_h, wq),
        (qry_h, qry), (key_h, key), (selq_h, selq), (rowq_h, rowq),
    )
    fetch = [pltpu.make_async_copy(a, b, loads.at[i]) for i, (a, b) in enumerate(pairs)]
    for copy in fetch:
        copy.start()

    barrier = pltpu.get_barrier_semaphore()

    def hello(dev):
        pl.semaphore_signal(barrier, inc=1, device_id={"seq": dev}, device_id_type=pl.DeviceIdType.MESH)

    for d in range(1, TEAM):
        hello(peer(d))
    pl.when(has_prev)(lambda: hello(me - 1))
    pl.when(has_next)(lambda: hello(me + 1))
    pl.when(has_up)(lambda: hello(me - TEAM))
    pl.when(has_down)(lambda: hello(me + TEAM))
    greeted = TEAM - 1
    for there in (has_prev, has_next, has_up, has_down):
        greeted = greeted + there.astype(jnp.int32)
    pl.semaphore_wait(barrier, greeted)

    def remote(src, dst, send, recv, dev):
        return pltpu.make_async_remote_copy(
            src_ref=src, dst_ref=dst, send_sem=send, recv_sem=recv,
            device_id={"seq": dev}, device_id_type=pl.DeviceIdType.MESH,
        )

    tail_copy = remote(hid_h.at[pl.ds(count - 16, 16)], hprev, hs_send.at[0], hs_recv.at[0], me + 1)
    key_copy = remote(key_h.at[pl.ds(count - WINDOW, WINDOW)], kprev, hs_send.at[1], hs_recv.at[1], me + 1)
    val_copy = remote(cv.at[pl.ds(count - WINDOW, WINDOW)], vprev, hs_send.at[2], hs_recv.at[2], me + 1)

    @pl.when(has_next)
    def _():
        tail_copy.start()
        key_copy.start()

    @pl.when(jnp.logical_not(has_prev))
    def _():
        hprev[...] = jnp.zeros_like(hprev)
        kprev[...] = jnp.zeros_like(kprev)
        vprev[...] = jnp.zeros_like(vprev)

    r = lax.broadcasted_iota(jnp.int32, (count, head), 0)
    j = lax.broadcasted_iota(jnp.int32, (count, head), 1)
    rr = lax.rem(r, WINDOW)
    first = jnp.where(has_prev, 0, WINDOW)
    ok = (j > rr) & (j <= rr + WINDOW) & ((j >= first) | (r >= WINDOW))
    wbias[...] = jnp.where(ok, 0.0, -1e30)
    half = count // 2
    r = lax.broadcasted_iota(jnp.int32, (half, half), 0)
    j = lax.broadcasted_iota(jnp.int32, (half, half), 1)
    cmask[...] = jnp.where(j <= r, 1.0, 0.0)

    for copy in fetch[:4]:
        copy.wait()
    pl.when(has_prev)(lambda: tail_copy.wait_recv())

    wide = 2 * head
    row = lax.broadcasted_iota(jnp.int32, (count, wide), 0)

    def conv_step(b, c):
        cols = pl.ds(pl.multiple_of(b * wide, wide), wide)
        h = hid[:, cols].astype(F32)
        hp = hprev[:, cols].astype(F32)
        w = cw[:, cols]
        h1 = jnp.where(row == 0, hp[15:16], pltpu.roll(h, 1, 0))
        h2 = jnp.where(row == 0, hp[14:15], jnp.where(row == 1, hp[15:16], pltpu.roll(h, 2, 0)))
        cv[:, cols] = (w[0:1] * h2 + w[1:2] * h1 + w[2:3] * h).astype(BF)
        return c

    lax.fori_loop(0, width // wide, conv_step, 0)
    pl.when(has_next)(lambda: val_copy.start())

    fk = nn(cv[...], wk[...]).astype(BF).astype(F32)
    fkt[...] = fk.T.astype(BF)

    trow = lax.broadcasted_iota(jnp.int32, (16, count), 0)
    pick_a = jnp.where(trow == 9, 1.0, 0.0).astype(BF)
    pick_b = jnp.where(trow == 10, 1.0, 0.0).astype(BF)
    ones_k = jnp.ones((FEAT, count), BF)
    zeros_k = jnp.zeros((256 - ROWS, count), BF)

    def state_step(h):
        x = jnp.concatenate([fkt[pl.ds(pl.multiple_of(h * FEAT, FEAT), FEAT), :], ones_k], axis=0)
        ab = nn(selk[...], x)
        p = ab[:ROWS] * ab[ROWS:]
        p = jnp.concatenate([p[:QUADS] * C2, p[QUADS:]], axis=0).astype(BF)
        v = cv[:, pl.ds(pl.multiple_of(h * head, head), head)]
        s = nn(p, v)
        tail = s[144:] + nt(pick_a, p[:128]) + nt(pick_b, jnp.concatenate([p[128:], zeros_k], axis=0))
        st[h] = jnp.concatenate([s[:144], tail], axis=0).astype(BF)

    each = per // CHUNKS

    def to_owner(c, d):
        heads = pl.ds(lax.rem(pos + d, TEAM) * per + c * each, each)
        return remote(
            st.at[heads], rbuf.at[pos, pl.ds(c * each, each)], a_send.at[c, d], a_recv.at[c, d], peer(d)
        )

    for c in range(CHUNKS):

        def for_peer(d, carry, c=c):
            h = lax.rem(pos + d, TEAM) * per + c * each
            for k in range(each):
                state_step(h + k)
            pl.when(d < TEAM)(lambda: to_owner(c, d).start())
            return carry

        lax.fori_loop(1, TEAM + 1, for_peer, 0)

    fetch[4].wait()
    fq = nn(cv[...], wq[...]).astype(BF)
    for b in range(2):
        fqs[b] = fq[:, b * 128 : (b + 1) * 128]

    ones_v = jnp.ones((count, head), BF)
    lane = lax.broadcasted_iota(jnp.int32, (8, 128), 1)

    def masked_query(h):
        mask = jnp.where(lane // FEAT == lax.rem(h, 8), 1.0, 0.0)[0:1].astype(BF)
        return fqs[h // 8] * mask

    lin, sq = FEAT**-0.5, 0.5 / FEAT

    def local_step(h):
        cols = pl.ds(pl.multiple_of(h * head, head), head)
        q = qry[:, cols]
        k = jnp.concatenate([kprev[:, cols], key[:, cols]], axis=0)
        v = cv[:, cols]
        ve = jnp.concatenate([vprev[:, cols], v], axis=0)
        s = jnp.concatenate(
            [nt(q[i : i + WINDOW], k[i : i + 2 * WINDOW]) for i in range(0, count, WINDOW)], axis=0
        )
        s = s * head**-0.5 + wbias[...]
        w = jnp.exp(s - jnp.max(s, axis=-1, keepdims=True)).astype(BF)
        va = jnp.concatenate([ve, jnp.ones_like(ve)], axis=1)
        y = jnp.concatenate(
            [nn(w[i : i + WINDOW], va[i : i + 2 * WINDOW]) for i in range(0, count, WINDOW)], axis=0
        )
        ywin[:, cols] = y[:, :head] / y[:, head:]
        fqm = masked_query(h)
        kt = fkt[pl.ds(pl.multiple_of((h // 8) * 128, 128), 128), :]
        vb = jnp.concatenate([v, ones_v], axis=1)
        x = nn(fqm[:half], kt[:, :half])
        a = ((1.0 + x * (lin + sq * x)) * cmask[...]).astype(BF)
        na = nn(a, vb[:half])
        num[:half, cols] = na[:, :head]
        den[:half, cols] = na[:, head:]
        x = nn(fqm[half:], kt)
        a = 1.0 + x * (lin + sq * x)
        a = jnp.concatenate([a[:, :half], a[:, half:] * cmask[...]], axis=1).astype(BF)
        na = nn(a, vb)
        num[half:, cols] = na[:, :head]
        den[half:, cols] = na[:, head:]

    def chain(c):
        part = pl.ds(c * each, each)
        return remote(cout.at[part], cin.at[part], c_send.at[c], c_recv.at[c], me + TEAM)

    def to_user(c, d):
        part = pl.ds(c * each, each)
        return remote(obuf.at[d, part], sbuf.at[pos, part], b_send.at[c, d], b_recv.at[c, d], peer(d))

    def pass_on(c):
        part = pl.ds(c * each, each)
        rbuf[pos, part] = st[pl.ds(pos * per + c * each, each)]
        for d in range(1, TEAM):
            to_owner(c, d).wait_recv()
        got = [rbuf[i, part].astype(F32) for i in range(TEAM)]
        pl.when(has_up)(lambda: chain(c).wait_recv())

        @pl.when(jnp.logical_not(has_up))
        def _():
            cin[part] = jnp.zeros_like(cin[part])

        base = cin[part].astype(F32)

        @pl.when(has_down)
        def _():
            cout[part] = (base + (got[0] + got[1] + got[2] + got[3])).astype(BF)
            chain(c).start()

        for d in (2, 3, 1, 0):
            target = lax.rem(pos + d, TEAM)
            acc = base
            for i in range(TEAM - 1):
                acc = acc + got[i] * jnp.where(i < target, 1.0, 0.0)
            if d == 0:
                sbuf[pos, part] = acc.astype(BF)
            else:
                obuf[d, part] = acc.astype(BF)
                to_user(c, d).start()

    for copy in fetch[5:]:
        copy.wait()
    pl.when(has_prev)(lambda: key_copy.wait_recv())
    pl.when(has_prev)(lambda: val_copy.wait_recv())

    steps = HEADS // 2
    turns = [jnp.minimum(TURN0 + TURNC * c + TURNT * team, steps) for c in range(CHUNKS)]

    def local_and_pass(i, carry):
        for c in range(CHUNKS):
            pl.when(i == turns[c])(functools.partial(pass_on, c))
        local_step(2 * i)
        local_step(2 * i + 1)
        return carry

    lax.fori_loop(0, steps, local_and_pass, 0)

    spare = jnp.zeros((256 - ROWS, head), BF)

    def final_step(h):
        cols = pl.ds(pl.multiple_of(h * head, head), head)
        lr = nn(masked_query(h), selq[...])
        ph = (((lr[:, :256] + rowq[0:1]) * (lr[:, 256:] + rowq[1:2])) * rowq[2:3]).astype(BF)
        s = sbuf[h // per, lax.rem(h, per)]
        t = s[144:].astype(F32)
        nrow = jnp.concatenate(
            [jnp.broadcast_to(t[9:10], (head, head)), jnp.broadcast_to(t[10:11], (head, head))], axis=1
        ).astype(BF)
        no = nn(ph, jnp.concatenate([s, spare], axis=0))
        do = nt(ph, nrow)
        y = ywin[:, cols] + (num[:, cols] + no) / (den[:, cols] + do)
        out[:, cols] = y.astype(BF)

    def finish(c, d):
        h = lax.rem(pos + TEAM - d, TEAM) * per + c * each
        for k in range(each):
            final_step(h + k)

    for c in range(CHUNKS):
        pl.when(turns[c] == steps)(functools.partial(pass_on, c))
        finish(c, 0)
    for c in range(CHUNKS):

        def from_owner(d, carry, c=c):
            to_user(c, d).wait_recv()
            finish(c, d)
            return carry

        lax.fori_loop(1, TEAM, from_owner, 0)

    @pl.when(has_next)
    def _():
        tail_copy.wait_send()
        key_copy.wait_send()
        val_copy.wait_send()

    for c in range(CHUNKS):
        for d in range(1, TEAM):
            to_owner(c, d).wait_send()
            to_user(c, d).wait_send()
        pl.when(has_down)(lambda c=c: chain(c).wait_send())


def local(n, hidden, conv_weight, feat_query_w, feat_key_w, win_query, win_key):
    count, width = hidden.shape
    head = width // HEADS
    per = HEADS // TEAM
    selk, selq, rowq = tables(128)
    quarter = (per, ROWS, head)
    dma = pltpu.SemaphoreType.DMA
    return pl.pallas_call(
        functools.partial(kernel, n),
        out_shape=jax.ShapeDtypeStruct((count, width), BF),
        in_specs=[pl.BlockSpec(memory_space=pl.ANY)] * 9,
        out_specs=pl.BlockSpec(memory_space=pltpu.VMEM),
        scratch_shapes=[
            pltpu.VMEM((count, width), BF),
            pltpu.VMEM(conv_weight.shape, F32),
            pltpu.VMEM(feat_query_w.shape, BF),
            pltpu.VMEM(feat_key_w.shape, BF),
            pltpu.VMEM((count, width), BF),
            pltpu.VMEM((count, width), BF),
            pltpu.VMEM(selk.shape, BF),
            pltpu.VMEM(selq.shape, BF),
            pltpu.VMEM(rowq.shape, F32),
            pltpu.VMEM((16, width), BF),
            pltpu.VMEM((WINDOW, width), BF),
            pltpu.VMEM((WINDOW, width), BF),
            pltpu.VMEM((count, width), BF),
            pltpu.VMEM((2, count, 128), BF),
            pltpu.VMEM((256, count), BF),
            pltpu.VMEM((HEADS, ROWS, head), BF),
            pltpu.VMEM((TEAM,) + quarter, BF),
            pltpu.VMEM(quarter, BF),
            pltpu.VMEM(quarter, BF),
            pltpu.VMEM((TEAM,) + quarter, BF),
            pltpu.VMEM((TEAM,) + quarter, BF),
            pltpu.VMEM((count, width), F32),
            pltpu.VMEM((count, width), F32),
            pltpu.VMEM((count, width), F32),
            pltpu.VMEM((count, head), F32),
            pltpu.VMEM((count // 2, count // 2), F32),
            dma((9,)), dma((3,)), dma((3,)), dma((CHUNKS, TEAM)), dma((CHUNKS, TEAM)),
            dma((CHUNKS,)), dma((CHUNKS,)), dma((CHUNKS, TEAM)), dma((CHUNKS, TEAM)),
        ],
        compiler_params=pltpu.CompilerParams(
            collective_id=0, has_side_effects=True, vmem_limit_bytes=56 * 1024 * 1024
        ),
    )(hidden, conv_weight, feat_query_w, feat_key_w, win_query, win_key, selk, selq, rowq)


def solution(mesh):
    placed = (P(("groups", "seq"), None), P(), P(), P(), P(("groups", "seq"), None), P(("groups", "seq"), None))
    return jax.shard_map(
        functools.partial(local, mesh.shape["seq"]),
        mesh=mesh, in_specs=placed, out_specs=P(("groups", "seq"), None), check_vma=False,
    )
```

```python
import functools

import jax
import jax.numpy as jnp
import numpy as np
from jax import lax
from jax.experimental import pallas as pl
from jax.experimental.pallas import tpu as pltpu
from jax.sharding import PartitionSpec as P

HEADS = 16
FEAT = 16
WINDOW = 64
TEAM = 4
CORES = 2
HALF = HEADS // CORES
ROWS = 160
QUADS = 136
CHUNKS = 4
PART = HALF // CHUNKS
TURN0 = 0
TURNC = 1
TURNT = 2
TURNB = 2
LAG = 3
LAGB = 1
C2 = (FEAT**-0.5) / 2.0**0.5
BF = jnp.bfloat16
F32 = jnp.float32


def tables(block):
    pairs = [(i, j) for i in range(FEAT) for j in range(i, FEAT)]
    left_k = np.zeros((2 * ROWS, 2 * FEAT), np.float32)
    reps = block // FEAT
    sel_q = np.zeros((FEAT, 512), np.float32)
    rows_q = np.zeros((8, 256), np.float32)
    for f, (i, j) in enumerate(pairs):
        left_k[f, i] = 1.0
        left_k[ROWS + f, j] = 1.0
        sel_q[i, f] = 1.0
        sel_q[j, 256 + f] = 1.0
        rows_q[2, f] = np.float32(C2) * (1.0 if i == j else 2.0)
    for i in range(FEAT):
        f = QUADS + i
        left_k[f, i] = 1.0
        left_k[ROWS + f, FEAT] = 0.5
        sel_q[i, f] = 1.0
        rows_q[1, f] = 0.5
        rows_q[2, f] = 1.0
    f = QUADS + FEAT
    left_k[f, FEAT] = 1.0
    left_k[ROWS + f, FEAT] = 1.0
    rows_q[0, f] = 1.0
    rows_q[1, f] = 1.0
    rows_q[2, f] = 1.0
    return jnp.asarray(left_k, BF), jnp.asarray(np.tile(sel_q, (reps, 1)), BF), jnp.asarray(rows_q, F32)


def nt(a, b):
    return lax.dot_general(a, b, (((1,), (1,)), ((), ())), preferred_element_type=F32)


def nn(a, b):
    return jnp.dot(a, b, preferred_element_type=F32)


def kernel(
    n, hid_h, cw_h, wq_h, wk_h, qry_h, key_h, selk_h, selq_h, rowq_h, out,
    hid, cw, wq, wk, qry, key, selk, selq, rowq,
    hprev, kprev, vprev, cv, fqs, fkt, st, rbuf, cin, cout, yin, obuf, sbuf,
    ywin, num, den, wbias, cmask,
    loads, hs_send, hs_recv, a_send, a_recv, c_send, c_recv, y_send, y_recv, b_send, b_recv,
):
    count, width = hid.shape
    head = width // HEADS
    me = lax.axis_index("seq")
    team = me // TEAM
    core = lax.rem(me, CORES)
    side = lax.rem(me // CORES, 2)
    teams = n // TEAM
    has_prev, has_next = me > 0, me < n - 1
    has_up, has_down = team > 0, team < teams - 1
    sibling = me + 1 - 2 * core
    across = me + CORES - 2 * CORES * side
    mine_at, theirs_at = core * HALF, (1 - core) * HALF

    pairs = (
        (hid_h, hid), (cw_h, cw), (wk_h, wk), (selk_h, selk), (wq_h, wq),
        (qry_h, qry), (key_h, key), (selq_h, selq), (rowq_h, rowq),
    )
    fetch = [pltpu.make_async_copy(a, b, loads.at[i]) for i, (a, b) in enumerate(pairs)]
    for copy in fetch:
        copy.start()

    barrier = pltpu.get_barrier_semaphore()

    def hello(dev):
        pl.semaphore_signal(barrier, inc=1, device_id={"seq": dev}, device_id_type=pl.DeviceIdType.MESH)

    hello(sibling)
    hello(across)
    pl.when(has_prev)(lambda: hello(me - 1))
    pl.when(has_next)(lambda: hello(me + 1))
    pl.when(has_up)(lambda: hello(me - TEAM))
    pl.when(has_down)(lambda: hello(me + TEAM))
    greeted = 2
    for there in (has_prev, has_next, has_up, has_down):
        greeted = greeted + there.astype(jnp.int32)
    pl.semaphore_wait(barrier, greeted)

    def remote(src, dst, send, recv, dev):
        return pltpu.make_async_remote_copy(
            src_ref=src, dst_ref=dst, send_sem=send, recv_sem=recv,
            device_id={"seq": dev}, device_id_type=pl.DeviceIdType.MESH,
        )

    tail_copy = remote(hid_h.at[pl.ds(count - 16, 16)], hprev, hs_send.at[0], hs_recv.at[0], me + 1)
    key_copy = remote(key_h.at[pl.ds(count - WINDOW, WINDOW)], kprev, hs_send.at[1], hs_recv.at[1], me + 1)
    val_copy = remote(cv.at[pl.ds(count - WINDOW, WINDOW)], vprev, hs_send.at[2], hs_recv.at[2], me + 1)

    @pl.when(has_next)
    def _():
        tail_copy.start()
        key_copy.start()

    @pl.when(jnp.logical_not(has_prev))
    def _():
        hprev[...] = jnp.zeros_like(hprev)
        kprev[...] = jnp.zeros_like(kprev)
        vprev[...] = jnp.zeros_like(vprev)

    r = lax.broadcasted_iota(jnp.int32, (count, head), 0)
    j = lax.broadcasted_iota(jnp.int32, (count, head), 1)
    rr = lax.rem(r, WINDOW)
    first = jnp.where(has_prev, 0, WINDOW)
    ok = (j > rr) & (j <= rr + WINDOW) & ((j >= first) | (r >= WINDOW))
    wbias[...] = jnp.where(ok, 0.0, -1e30)
    half = count // 2
    r = lax.broadcasted_iota(jnp.int32, (half, half), 0)
    j = lax.broadcasted_iota(jnp.int32, (half, half), 1)
    cmask[...] = jnp.where(j <= r, 1.0, 0.0)

    for copy in fetch[:4]:
        copy.wait()
    pl.when(has_prev)(lambda: tail_copy.wait_recv())

    wide = 2 * head
    row = lax.broadcasted_iota(jnp.int32, (count, wide), 0)

    def conv_step(b, c):
        cols = pl.ds(pl.multiple_of(b * wide, wide), wide)
        h = hid[:, cols].astype(F32)
        hp = hprev[:, cols].astype(F32)
        w = cw[:, cols]
        h1 = jnp.where(row == 0, hp[15:16], pltpu.roll(h, 1, 0))
        h2 = jnp.where(row == 0, hp[14:15], jnp.where(row == 1, hp[15:16], pltpu.roll(h, 2, 0)))
        cv[:, cols] = (w[0:1] * h2 + w[1:2] * h1 + w[2:3] * h).astype(BF)
        return c

    lax.fori_loop(0, width // wide, conv_step, 0)
    pl.when(has_next)(lambda: val_copy.start())

    fk = nn(cv[...], wk[...]).astype(BF).astype(F32)
    fkt[...] = fk.T.astype(BF)

    trow = lax.broadcasted_iota(jnp.int32, (16, count), 0)
    pick_a = jnp.where(trow == 9, 1.0, 0.0).astype(BF)
    pick_b = jnp.where(trow == 10, 1.0, 0.0).astype(BF)
    ones_k = jnp.ones((FEAT, count), BF)
    zeros_k = jnp.zeros((256 - ROWS, count), BF)

    def state_step(h):
        x = jnp.concatenate([fkt[pl.ds(pl.multiple_of(h * FEAT, FEAT), FEAT), :], ones_k], axis=0)
        ab = nn(selk[...], x)
        p = ab[:ROWS] * ab[ROWS:]
        p = jnp.concatenate([p[:QUADS] * C2, p[QUADS:]], axis=0).astype(BF)
        v = cv[:, pl.ds(pl.multiple_of(h * head, head), head)]
        s = nn(p, v)
        tail = s[144:] + nt(pick_a, p[:128]) + nt(pick_b, jnp.concatenate([p[128:], zeros_k], axis=0))
        st[h] = jnp.concatenate([s[:144], tail], axis=0).astype(BF)

    def to_sibling(k):
        return remote(
            st.at[pl.ds(theirs_at + k * PART, PART)], rbuf.at[pl.ds(k * PART, PART)],
            a_send.at[k], a_recv.at[k], sibling,
        )

    def states(k, carry):
        for i in range(PART):
            state_step(theirs_at + k * PART + i)
        to_sibling(k).start()
        for i in range(PART):
            state_step(mine_at + k * PART + i)
        return carry

    lax.fori_loop(0, CHUNKS, states, 0)

    fetch[4].wait()
    fq = nn(cv[...], wq[...]).astype(BF)
    for b in range(2):
        fqs[b] = fq[:, b * 128 : (b + 1) * 128]

    ones_v = jnp.ones((count, head), BF)
    lane = lax.broadcasted_iota(jnp.int32, (8, 128), 1)

    def masked_query(h):
        mask = jnp.where(lane // FEAT == lax.rem(h, 8), 1.0, 0.0)[0:1].astype(BF)
        return fqs[h // 8] * mask

    lin, sq = FEAT**-0.5, 0.5 / FEAT

    def local_step(h):
        cols = pl.ds(pl.multiple_of(h * head, head), head)
        q = qry[:, cols]
        k = jnp.concatenate([kprev[:, cols], key[:, cols]], axis=0)
        v = cv[:, cols]
        ve = jnp.concatenate([vprev[:, cols], v], axis=0)
        s = jnp.concatenate(
            [nt(q[i : i + WINDOW], k[i : i + 2 * WINDOW]) for i in range(0, count, WINDOW)], axis=0
        )
        s = s * head**-0.5 + wbias[...]
        w = jnp.exp(s - jnp.max(s, axis=-1, keepdims=True)).astype(BF)
        va = jnp.concatenate([ve, jnp.ones_like(ve)], axis=1)
        y = jnp.concatenate(
            [nn(w[i : i + WINDOW], va[i : i + 2 * WINDOW]) for i in range(0, count, WINDOW)], axis=0
        )
        ywin[:, cols] = y[:, :head] / y[:, head:]
        fqm = masked_query(h)
        kt = fkt[pl.ds(pl.multiple_of((h // 8) * 128, 128), 128), :]
        vb = jnp.concatenate([v, ones_v], axis=1)
        x = nn(fqm[:half], kt[:, :half])
        a = ((1.0 + x * (lin + sq * x)) * cmask[...]).astype(BF)
        na = nn(a, vb[:half])
        num[:half, cols] = na[:, :head]
        den[:half, cols] = na[:, head:]
        x = nn(fqm[half:], kt)
        a = 1.0 + x * (lin + sq * x)
        a = jnp.concatenate([a[:, :half], a[:, half:] * cmask[...]], axis=1).astype(BF)
        na = nn(a, vb)
        num[half:, cols] = na[:, :head]
        den[half:, cols] = na[:, head:]

    def chain(k):
        part = pl.ds(k * PART, PART)
        return remote(cout.at[part], cin.at[part], c_send.at[k], c_recv.at[k], me + TEAM)

    def cross(k, src):
        part = pl.ds(k * PART, PART)
        return remote(src.at[part], yin.at[part], y_send.at[k], y_recv.at[k], across)

    def back(k):
        return remote(
            obuf.at[pl.ds(k * PART, PART)], sbuf.at[pl.ds(mine_at + k * PART, PART)],
            b_send.at[k], b_recv.at[k], sibling,
        )

    def pass_on(k):
        part = pl.ds(k * PART, PART)
        to_sibling(k).wait_recv()
        both = st[pl.ds(mine_at + k * PART, PART)].astype(F32) + rbuf[part].astype(F32)
        pl.when(has_up)(lambda: chain(k).wait_recv())

        @pl.when(jnp.logical_not(has_up))
        def _():
            cin[part] = jnp.zeros_like(cin[part])

        cout[part] = (cin[part].astype(F32) + both).astype(BF)
        pl.when(has_down)(lambda: chain(k).start())
        pl.when(side == 0)(lambda: cross(k, cout).start())
        pl.when(side == 1)(lambda: cross(k, cin).start())

    own_first = jnp.where(core == 0, 1.0, 0.0)

    def give_back(k):
        part = pl.ds(k * PART, PART)
        cross(k, cin).wait_recv()
        before = cin[part].astype(F32) + yin[part].astype(F32)
        at = pl.ds(mine_at + k * PART, PART)
        obuf[part] = (before + own_first * st[at].astype(F32)).astype(BF)
        back(k).start()
        sbuf[at] = (before + (1.0 - own_first) * rbuf[part].astype(F32)).astype(BF)

    for copy in fetch[5:]:
        copy.wait()
    pl.when(has_prev)(lambda: key_copy.wait_recv())
    pl.when(has_prev)(lambda: val_copy.wait_recv())

    steps = HEADS // 2
    def turn(k):
        return jnp.minimum(TURN0 + TURNC * k + TURNT * team, steps)

    def turn_back(k):
        return jnp.minimum(turn(k) + TURNB, steps)

    def events(i):
        def one(k, carry):
            pl.when(i == turn(k))(lambda: pass_on(k))
            pl.when(i == turn_back(k))(lambda: give_back(k))
            return carry

        lax.fori_loop(0, CHUNKS, one, 0)

    def local_and_pass(i, carry):
        events(i)
        local_step(2 * i)
        local_step(2 * i + 1)
        return carry

    lax.fori_loop(0, steps, local_and_pass, 0)

    spare = jnp.zeros((256 - ROWS, head), BF)

    def final_step(h):
        cols = pl.ds(pl.multiple_of(h * head, head), head)
        lr = nn(masked_query(h), selq[...])
        ph = (((lr[:, :256] + rowq[0:1]) * (lr[:, 256:] + rowq[1:2])) * rowq[2:3]).astype(BF)
        s = sbuf[h]
        t = s[144:].astype(F32)
        nrow = jnp.concatenate(
            [jnp.broadcast_to(t[9:10], (head, head)), jnp.broadcast_to(t[10:11], (head, head))], axis=1
        ).astype(BF)
        no = nn(ph, jnp.concatenate([s, spare], axis=0))
        do = nt(ph, nrow)
        y = ywin[:, cols] + (num[:, cols] + no) / (den[:, cols] + do)
        out[:, cols] = y.astype(BF)

    def wind_up(k, carry):
        @pl.when(k < CHUNKS)
        def _():
            pl.when(turn(k) == steps)(lambda: pass_on(k))

        @pl.when((k >= LAG) & (k < CHUNKS + LAG))
        def _():
            pl.when(turn_back(k - LAG) == steps)(lambda: give_back(k - LAG))
            for i in range(PART):
                final_step(mine_at + (k - LAG) * PART + i)

        @pl.when(k >= LAG + LAGB)
        def _():
            back(k - LAG - LAGB).wait_recv()
            for i in range(PART):
                final_step(theirs_at + (k - LAG - LAGB) * PART + i)

        return carry

    lax.fori_loop(0, CHUNKS + LAG + LAGB, wind_up, 0)

    @pl.when(has_next)
    def _():
        tail_copy.wait_send()
        key_copy.wait_send()
        val_copy.wait_send()

    for k in range(CHUNKS):
        to_sibling(k).wait_send()
        cross(k, cin).wait_send()
        back(k).wait_send()
        pl.when(has_down)(lambda k=k: chain(k).wait_send())


def local(n, hidden, conv_weight, feat_query_w, feat_key_w, win_query, win_key):
    count, width = hidden.shape
    head = width // HEADS
    selk, selq, rowq = tables(128)
    half = (HALF, ROWS, head)
    dma = pltpu.SemaphoreType.DMA
    return pl.pallas_call(
        functools.partial(kernel, n),
        out_shape=jax.ShapeDtypeStruct((count, width), BF),
        in_specs=[pl.BlockSpec(memory_space=pl.ANY)] * 9,
        out_specs=pl.BlockSpec(memory_space=pltpu.VMEM),
        scratch_shapes=[
            pltpu.VMEM((count, width), BF),
            pltpu.VMEM(conv_weight.shape, F32),
            pltpu.VMEM(feat_query_w.shape, BF),
            pltpu.VMEM(feat_key_w.shape, BF),
            pltpu.VMEM((count, width), BF),
            pltpu.VMEM((count, width), BF),
            pltpu.VMEM(selk.shape, BF),
            pltpu.VMEM(selq.shape, BF),
            pltpu.VMEM(rowq.shape, F32),
            pltpu.VMEM((16, width), BF),
            pltpu.VMEM((WINDOW, width), BF),
            pltpu.VMEM((WINDOW, width), BF),
            pltpu.VMEM((count, width), BF),
            pltpu.VMEM((2, count, 128), BF),
            pltpu.VMEM((256, count), BF),
            pltpu.VMEM((HEADS, ROWS, head), BF),
            pltpu.VMEM(half, BF),
            pltpu.VMEM(half, BF),
            pltpu.VMEM(half, BF),
            pltpu.VMEM(half, BF),
            pltpu.VMEM(half, BF),
            pltpu.VMEM((HEADS, ROWS, head), BF),
            pltpu.VMEM((count, width), F32),
            pltpu.VMEM((count, width), F32),
            pltpu.VMEM((count, width), F32),
            pltpu.VMEM((count, head), F32),
            pltpu.VMEM((count // 2, count // 2), F32),
            dma((9,)), dma((3,)), dma((3,)),
        ]
        + [dma((CHUNKS,))] * 8,
        compiler_params=pltpu.CompilerParams(
            collective_id=0, has_side_effects=True, vmem_limit_bytes=56 * 1024 * 1024
        ),
    )(hidden, conv_weight, feat_query_w, feat_key_w, win_query, win_key, selk, selq, rowq)


def solution(mesh):
    placed = (P(("groups", "seq"), None), P(), P(), P(), P(("groups", "seq"), None), P(("groups", "seq"), None))
    return jax.shard_map(
        functools.partial(local, mesh.shape["seq"]),
        mesh=mesh, in_specs=placed, out_specs=P(("groups", "seq"), None), check_vma=False,
    )
```

```python
import functools

import jax
import jax.numpy as jnp
import numpy as np
from jax import lax
from jax.experimental import pallas as pl
from jax.experimental.pallas import tpu as pltpu
from jax.sharding import PartitionSpec as P

HEADS = 16
FEAT = 16
WINDOW = 64
TEAM = 4
CORES = 2
HALF = HEADS // CORES
ROWS = 160
QUADS = 136
CHUNKS = 4
PART = HALF // CHUNKS
TURN0 = -1
TURNC = 1
TURNT = 2
TURNB = 2
LAG = 3
LAGB = 1
C2 = (FEAT**-0.5) / 2.0**0.5
BF = jnp.bfloat16
F32 = jnp.float32


def tables(block):
    pairs = [(i, j) for i in range(FEAT) for j in range(i, FEAT)]
    left_k = np.zeros((2 * ROWS, 2 * FEAT), np.float32)
    reps = block // FEAT
    sel_q = np.zeros((FEAT, 512), np.float32)
    rows_q = np.zeros((8, 256), np.float32)
    for f, (i, j) in enumerate(pairs):
        left_k[f, i] = 1.0
        left_k[ROWS + f, j] = 1.0
        sel_q[i, f] = 1.0
        sel_q[j, 256 + f] = 1.0
        rows_q[2, f] = np.float32(C2) * (1.0 if i == j else 2.0)
    for i in range(FEAT):
        f = QUADS + i
        left_k[f, i] = 1.0
        left_k[ROWS + f, FEAT] = 0.5
        sel_q[i, f] = 1.0
        rows_q[1, f] = 0.5
        rows_q[2, f] = 1.0
    f = QUADS + FEAT
    left_k[f, FEAT] = 1.0
    left_k[ROWS + f, FEAT] = 1.0
    rows_q[0, f] = 1.0
    rows_q[1, f] = 1.0
    rows_q[2, f] = 1.0
    return jnp.asarray(left_k, BF), jnp.asarray(np.tile(sel_q, (reps, 1)), BF), jnp.asarray(rows_q, F32)


def nt(a, b):
    return lax.dot_general(a, b, (((1,), (1,)), ((), ())), preferred_element_type=F32)


def nn(a, b):
    return jnp.dot(a, b, preferred_element_type=F32)


def kernel(
    n, hid_h, cw_h, wq_h, wk_h, qry_h, key_h, selk_h, selq_h, rowq_h, out,
    hid, cw, wq, wk, qry, key, selk, selq, rowq,
    hprev, kprev, vprev, cv, fqs, fkt, st, rbuf, cin, cout, yin, obuf, sbuf,
    ywin, num, den, wbias, cmask,
    loads, hs_send, hs_recv, a_send, a_recv, c_send, c_recv, y_send, y_recv, b_send, b_recv,
):
    count, width = hid.shape
    head = width // HEADS
    me = lax.axis_index("seq")
    team = me // TEAM
    core = lax.rem(me, CORES)
    side = lax.rem(me // CORES, 2)
    teams = n // TEAM
    has_prev, has_next = me > 0, me < n - 1
    has_up, has_down = team > 0, team < teams - 1
    sibling = me + 1 - 2 * core
    across = me + CORES - 2 * CORES * side
    mine_at, theirs_at = core * HALF, (1 - core) * HALF

    pairs = (
        (hid_h, hid), (cw_h, cw), (wk_h, wk), (selk_h, selk), (wq_h, wq),
        (qry_h, qry), (key_h, key), (selq_h, selq), (rowq_h, rowq),
    )
    fetch = [pltpu.make_async_copy(a, b, loads.at[i]) for i, (a, b) in enumerate(pairs)]
    for copy in fetch:
        copy.start()

    barrier = pltpu.get_barrier_semaphore()

    def hello(dev):
        pl.semaphore_signal(barrier, inc=1, device_id={"seq": dev}, device_id_type=pl.DeviceIdType.MESH)

    hello(sibling)
    hello(across)
    pl.when(has_prev)(lambda: hello(me - 1))
    pl.when(has_next)(lambda: hello(me + 1))
    pl.when(has_up)(lambda: hello(me - TEAM))
    pl.when(has_down)(lambda: hello(me + TEAM))
    greeted = 2
    for there in (has_prev, has_next, has_up, has_down):
        greeted = greeted + there.astype(jnp.int32)
    pl.semaphore_wait(barrier, greeted)

    def remote(src, dst, send, recv, dev):
        return pltpu.make_async_remote_copy(
            src_ref=src, dst_ref=dst, send_sem=send, recv_sem=recv,
            device_id={"seq": dev}, device_id_type=pl.DeviceIdType.MESH,
        )

    tail_copy = remote(hid_h.at[pl.ds(count - 16, 16)], hprev, hs_send.at[0], hs_recv.at[0], me + 1)
    key_copy = remote(key_h.at[pl.ds(count - WINDOW, WINDOW)], kprev, hs_send.at[1], hs_recv.at[1], me + 1)
    val_copy = remote(cv.at[pl.ds(count - WINDOW, WINDOW)], vprev, hs_send.at[2], hs_recv.at[2], me + 1)

    @pl.when(has_next)
    def _():
        tail_copy.start()
        key_copy.start()

    @pl.when(jnp.logical_not(has_prev))
    def _():
        hprev[...] = jnp.zeros_like(hprev)
        kprev[...] = jnp.zeros_like(kprev)
        vprev[...] = jnp.zeros_like(vprev)

    r = lax.broadcasted_iota(jnp.int32, (count, head), 0)
    j = lax.broadcasted_iota(jnp.int32, (count, head), 1)
    rr = lax.rem(r, WINDOW)
    first = jnp.where(has_prev, 0, WINDOW)
    ok = (j > rr) & (j <= rr + WINDOW) & ((j >= first) | (r >= WINDOW))
    wbias[...] = jnp.where(ok, 0.0, -1e30)
    half = count // 2
    r = lax.broadcasted_iota(jnp.int32, (half, half), 0)
    j = lax.broadcasted_iota(jnp.int32, (half, half), 1)
    cmask[...] = jnp.where(j <= r, 1.0, 0.0)

    for copy in fetch[:4]:
        copy.wait()
    pl.when(has_prev)(lambda: tail_copy.wait_recv())

    wide = 2 * head
    row = lax.broadcasted_iota(jnp.int32, (count, wide), 0)

    def conv_step(b, c):
        cols = pl.ds(pl.multiple_of(b * wide, wide), wide)
        h = hid[:, cols].astype(F32)
        hp = hprev[:, cols].astype(F32)
        w = cw[:, cols]
        h1 = jnp.where(row == 0, hp[15:16], pltpu.roll(h, 1, 0))
        h2 = jnp.where(row == 0, hp[14:15], jnp.where(row == 1, hp[15:16], pltpu.roll(h, 2, 0)))
        cv[:, cols] = (w[0:1] * h2 + w[1:2] * h1 + w[2:3] * h).astype(BF)
        return c

    lax.fori_loop(0, width // wide, conv_step, 0)
    pl.when(has_next)(lambda: val_copy.start())

    fk = nn(cv[...], wk[...]).astype(BF).astype(F32)
    fkt[...] = fk.T.astype(BF)

    trow = lax.broadcasted_iota(jnp.int32, (16, count), 0)
    pick_a = jnp.where(trow == 9, 1.0, 0.0).astype(BF)
    pick_b = jnp.where(trow == 10, 1.0, 0.0).astype(BF)
    ones_k = jnp.ones((FEAT, count), BF)
    zeros_k = jnp.zeros((256 - ROWS, count), BF)

    def state_step(h):
        x = jnp.concatenate([fkt[pl.ds(pl.multiple_of(h * FEAT, FEAT), FEAT), :], ones_k], axis=0)
        ab = nn(selk[...], x)
        p = ab[:ROWS] * ab[ROWS:]
        p = jnp.concatenate([p[:QUADS] * C2, p[QUADS:]], axis=0).astype(BF)
        v = cv[:, pl.ds(pl.multiple_of(h * head, head), head)]
        s = nn(p, v)
        tail = s[144:] + nt(pick_a, p[:128]) + nt(pick_b, jnp.concatenate([p[128:], zeros_k], axis=0))
        st[h] = jnp.concatenate([s[:144], tail], axis=0).astype(BF)

    def to_sibling(k):
        return remote(
            st.at[pl.ds(theirs_at + k * PART, PART)], rbuf.at[pl.ds(k * PART, PART)],
            a_send.at[k], a_recv.at[k], sibling,
        )

    def chain(k):
        part = pl.ds(k * PART, PART)
        return remote(cout.at[part], cin.at[part], c_send.at[k], c_recv.at[k], me + TEAM)

    def cross(k, src):
        part = pl.ds(k * PART, PART)
        return remote(src.at[part], yin.at[part], y_send.at[k], y_recv.at[k], across)

    def back(k):
        return remote(
            obuf.at[pl.ds(k * PART, PART)], sbuf.at[pl.ds(mine_at + k * PART, PART)],
            b_send.at[k], b_recv.at[k], sibling,
        )

    def pass_on(k):
        part = pl.ds(k * PART, PART)
        to_sibling(k).wait_recv()
        both = st[pl.ds(mine_at + k * PART, PART)].astype(F32) + rbuf[part].astype(F32)
        pl.when(has_up)(lambda: chain(k).wait_recv())

        @pl.when(jnp.logical_not(has_up))
        def _():
            cin[part] = jnp.zeros_like(cin[part])

        cout[part] = (cin[part].astype(F32) + both).astype(BF)
        pl.when(has_down)(lambda: chain(k).start())
        pl.when(side == 0)(lambda: cross(k, cout).start())
        pl.when(side == 1)(lambda: cross(k, cin).start())

    def states(k, carry):
        for i in range(PART):
            state_step(theirs_at + k * PART + i)
        to_sibling(k).start()
        for i in range(PART):
            state_step(mine_at + k * PART + i)
        pl.when(jnp.logical_not(has_up) & (k >= 1))(lambda: pass_on(k - 1))
        return carry

    lax.fori_loop(0, CHUNKS, states, 0)

    fetch[4].wait()
    fq = nn(cv[...], wq[...]).astype(BF)
    for b in range(2):
        fqs[b] = fq[:, b * 128 : (b + 1) * 128]
    pl.when(jnp.logical_not(has_up))(lambda: pass_on(CHUNKS - 1))

    ones_v = jnp.ones((count, head), BF)
    lane = lax.broadcasted_iota(jnp.int32, (8, 128), 1)

    def masked_query(h):
        mask = jnp.where(lane // FEAT == lax.rem(h, 8), 1.0, 0.0)[0:1].astype(BF)
        return fqs[h // 8] * mask

    lin, sq = FEAT**-0.5, 0.5 / FEAT

    def local_step(h):
        cols = pl.ds(pl.multiple_of(h * head, head), head)
        q = qry[:, cols]
        k = jnp.concatenate([kprev[:, cols], key[:, cols]], axis=0)
        v = cv[:, cols]
        ve = jnp.concatenate([vprev[:, cols], v], axis=0)
        s = jnp.concatenate(
            [nt(q[i : i + WINDOW], k[i : i + 2 * WINDOW]) for i in range(0, count, WINDOW)], axis=0
        )
        s = s * head**-0.5 + wbias[...]
        w = jnp.exp(s - jnp.max(s, axis=-1, keepdims=True)).astype(BF)
        va = jnp.concatenate([ve, jnp.ones_like(ve)], axis=1)
        y = jnp.concatenate(
            [nn(w[i : i + WINDOW], va[i : i + 2 * WINDOW]) for i in range(0, count, WINDOW)], axis=0
        )
        ywin[:, cols] = y[:, :head] / y[:, head:]
        fqm = masked_query(h)
        kt = fkt[pl.ds(pl.multiple_of((h // 8) * 128, 128), 128), :]
        vb = jnp.concatenate([v, ones_v], axis=1)
        x = nn(fqm[:half], kt[:, :half])
        a = ((1.0 + x * (lin + sq * x)) * cmask[...]).astype(BF)
        na = nn(a, vb[:half])
        num[:half, cols] = na[:, :head]
        den[:half, cols] = na[:, head:]
        x = nn(fqm[half:], kt)
        a = 1.0 + x * (lin + sq * x)
        a = jnp.concatenate([a[:, :half], a[:, half:] * cmask[...]], axis=1).astype(BF)
        na = nn(a, vb)
        num[half:, cols] = na[:, :head]
        den[half:, cols] = na[:, head:]

    own_first = jnp.where(core == 0, 1.0, 0.0)

    def give_back(k):
        part = pl.ds(k * PART, PART)
        cross(k, cin).wait_recv()
        before = cin[part].astype(F32) + yin[part].astype(F32)
        at = pl.ds(mine_at + k * PART, PART)
        obuf[part] = (before + own_first * st[at].astype(F32)).astype(BF)
        back(k).start()
        sbuf[at] = (before + (1.0 - own_first) * rbuf[part].astype(F32)).astype(BF)

    for copy in fetch[5:]:
        copy.wait()
    pl.when(has_prev)(lambda: key_copy.wait_recv())
    pl.when(has_prev)(lambda: val_copy.wait_recv())

    steps = HEADS // 2
    def turn(k):
        return jnp.where(has_up, jnp.minimum(TURN0 + TURNC * k + TURNT * team, steps), -1)

    def turn_back(k):
        return jnp.minimum(TURN0 + TURNC * k + TURNT * team + TURNB, steps)

    def events(i):
        def one(k, carry):
            pl.when(i == turn(k))(lambda: pass_on(k))
            pl.when(i == turn_back(k))(lambda: give_back(k))
            return carry

        lax.fori_loop(0, CHUNKS, one, 0)

    def local_and_pass(i, carry):
        events(i)
        local_step(2 * i)
        local_step(2 * i + 1)
        return carry

    lax.fori_loop(0, steps, local_and_pass, 0)

    spare = jnp.zeros((256 - ROWS, head), BF)

    def final_step(h):
        cols = pl.ds(pl.multiple_of(h * head, head), head)
        lr = nn(masked_query(h), selq[...])
        ph = (((lr[:, :256] + rowq[0:1]) * (lr[:, 256:] + rowq[1:2])) * rowq[2:3]).astype(BF)
        s = sbuf[h]
        t = s[144:].astype(F32)
        nrow = jnp.concatenate(
            [jnp.broadcast_to(t[9:10], (head, head)), jnp.broadcast_to(t[10:11], (head, head))], axis=1
        ).astype(BF)
        no = nn(ph, jnp.concatenate([s, spare], axis=0))
        do = nt(ph, nrow)
        y = ywin[:, cols] + (num[:, cols] + no) / (den[:, cols] + do)
        out[:, cols] = y.astype(BF)

    def wind_up(k, carry):
        @pl.when(k < CHUNKS)
        def _():
            pl.when(turn(k) == steps)(lambda: pass_on(k))

        @pl.when((k >= LAG) & (k < CHUNKS + LAG))
        def _():
            pl.when(turn_back(k - LAG) == steps)(lambda: give_back(k - LAG))
            for i in range(PART):
                final_step(mine_at + (k - LAG) * PART + i)

        @pl.when(k >= LAG + LAGB)
        def _():
            back(k - LAG - LAGB).wait_recv()
            for i in range(PART):
                final_step(theirs_at + (k - LAG - LAGB) * PART + i)

        return carry

    lax.fori_loop(0, CHUNKS + LAG + LAGB, wind_up, 0)

    @pl.when(has_next)
    def _():
        tail_copy.wait_send()
        key_copy.wait_send()
        val_copy.wait_send()

    for k in range(CHUNKS):
        to_sibling(k).wait_send()
        cross(k, cin).wait_send()
        back(k).wait_send()
        pl.when(has_down)(lambda k=k: chain(k).wait_send())


def local(n, hidden, conv_weight, feat_query_w, feat_key_w, win_query, win_key):
    count, width = hidden.shape
    head = width // HEADS
    selk, selq, rowq = tables(128)
    half = (HALF, ROWS, head)
    dma = pltpu.SemaphoreType.DMA
    return pl.pallas_call(
        functools.partial(kernel, n),
        out_shape=pltpu.VMEM((count, width), BF),
        in_specs=[pl.BlockSpec(memory_space=pl.ANY)] * 9,
        out_specs=pl.BlockSpec(memory_space=pltpu.VMEM),
        scratch_shapes=[
            pltpu.VMEM((count, width), BF),
            pltpu.VMEM(conv_weight.shape, F32),
            pltpu.VMEM(feat_query_w.shape, BF),
            pltpu.VMEM(feat_key_w.shape, BF),
            pltpu.VMEM((count, width), BF),
            pltpu.VMEM((count, width), BF),
            pltpu.VMEM(selk.shape, BF),
            pltpu.VMEM(selq.shape, BF),
            pltpu.VMEM(rowq.shape, F32),
            pltpu.VMEM((16, width), BF),
            pltpu.VMEM((WINDOW, width), BF),
            pltpu.VMEM((WINDOW, width), BF),
            pltpu.VMEM((count, width), BF),
            pltpu.VMEM((2, count, 128), BF),
            pltpu.VMEM((256, count), BF),
            pltpu.VMEM((HEADS, ROWS, head), BF),
            pltpu.VMEM(half, BF),
            pltpu.VMEM(half, BF),
            pltpu.VMEM(half, BF),
            pltpu.VMEM(half, BF),
            pltpu.VMEM(half, BF),
            pltpu.VMEM((HEADS, ROWS, head), BF),
            pltpu.VMEM((count, width), F32),
            pltpu.VMEM((count, width), F32),
            pltpu.VMEM((count, width), F32),
            pltpu.VMEM((count, head), F32),
            pltpu.VMEM((count // 2, count // 2), F32),
            dma((9,)), dma((3,)), dma((3,)),
        ]
        + [dma((CHUNKS,))] * 8,
        compiler_params=pltpu.CompilerParams(
            collective_id=0, has_side_effects=True, vmem_limit_bytes=56 * 1024 * 1024
        ),
    )(hidden, conv_weight, feat_query_w, feat_key_w, win_query, win_key, selk, selq, rowq)


def solution(mesh):
    placed = (P(("groups", "seq"), None), P(), P(), P(), P(("groups", "seq"), None), P(("groups", "seq"), None))
    return jax.shard_map(
        functools.partial(local, mesh.shape["seq"]),
        mesh=mesh, in_specs=placed, out_specs=P(("groups", "seq"), None), check_vma=False,
    )
```
